32 devices in a mesh: wide: 8 (over z, y), narrow: 4 (over x, core).
Axes of the slice: x: 2, y: 2, z: 4, core: 2. Of those that a mesh axis runs over, the one named last changes fastest.
Arguments:
- amplitudes: float32 [8, 64, 256, 256], P('wide', 'narrow'), may hold values from -6 to 6
- driver: float32 [8, 64, 256, 256], P('wide', 'narrow'), may hold values from -15 to 15
- fit_vectors: float32 [64, 1024, 256], P('narrow', 'wide'), may hold values from -0.09375 to 0.09375
- ladder_factors: float32 [2, 256, 256], P(None, 'wide'), may hold values from -0.25 to 0.25
- row_energy: float32 [8], P('wide'), may hold values from -2 to -0.3
- occupied_energy: float32 [64], P('narrow'), may hold values from -2 to -0.3
- virtual_energy: float32 [256], replicated, may hold values from 0.5 to 3
Outputs:
- updated: float32 [8, 64, 256, 256], P('wide', 'narrow')
The draws below stay inside these ranges and needn't reach their ends.
All inputs are finite; a program needn't handle non-finite values.
Results may differ from the reference program's by a relative error of at most 0.0001.
Values sent between devices are 32-bit elements; how exact they have to be, the bound alone decides.
A program may use at most 128 MiB of HBM per device.

```python
import jax
import jax.numpy as jnp
from jax import lax

O = 64
V = 256
NQ = 1024
NL = 2
ITERS = 2
NI = 8


def block_levels(own_key, dims, cuts, smallest, top_value):
    loudness = 1.0
    for dim, blocks in cuts:
        steps = jax.random.uniform(jax.random.fold_in(jax.random.fold_in(own_key, 6), dim), (blocks,), jnp.float32, smallest / len(cuts), top_value / len(cuts))
        loudness = loudness * jnp.repeat(jnp.exp(steps), dims[dim] // blocks).reshape((-1,) + (1,) * (len(dims) - 1 - dim))
    return loudness


def normal_values(key, shape, scale, most, cuts=(), held_as=jnp.bfloat16):
    values = jax.random.normal(key, shape, jnp.float32) * scale
    if len(cuts) > 0:
        values = block_levels(key, shape, cuts, -0.22, 0.18) * values
    return jnp.clip(values, min=-most, max=most).astype(held_as)


def setup_inputs(seed: int = 0) -> dict:
    arg_keys = jax.random.split(jax.random.key(seed), 8)
    return {
        "amplitudes": normal_values(arg_keys[0], (NI, O, V, V), 1.0, 6.0, ((0, 8), (1, 4)), jnp.float32),
        "driver": normal_values(arg_keys[1], (NI, O, V, V), 3.0, 15.0, ((0, 8), (1, 4)), jnp.float32),
        "fit_vectors": normal_values(arg_keys[2], (O, NQ, V), (O * V // 4) ** -0.5, 0.09375, ((0, 4), (1, 8)), jnp.float32),
        "ladder_factors": normal_values(arg_keys[3], (NL, V, V), (2 * V) ** -0.5, 0.25, ((1, 8),), jnp.float32),
        "row_energy": jnp.clip(-2.0 + 1.7 * jax.random.uniform(arg_keys[4], (NI,), jnp.float32) ** block_levels(arg_keys[4], (NI,), ((0, 8),), -0.2, 0.2), -2.0, -0.3),
        "occupied_energy": jnp.clip(-2.0 + 1.7 * jax.random.uniform(arg_keys[5], (O,), jnp.float32) ** block_levels(arg_keys[5], (O,), ((0, 4),), -0.2, 0.2), -2.0, -0.3),
        "virtual_energy": jnp.clip(jax.random.uniform(arg_keys[6], (V,), jnp.float32, 0.5, 3.0), 0.5, 3.0),
    }


def reference(amplitudes, driver, fit_vectors, ladder_factors, row_energy, occupied_energy, virtual_energy):
    highest = lax.Precision.HIGHEST
    pair_energy = virtual_energy[:, None] + virtual_energy[None, :]

    def update_row(operands):
        row_amps, row_driver, energy = operands
        denominator = pair_energy[None, :, :] - energy - occupied_energy[:, None, None]
        for iteration in range(ITERS):
            fitted = jnp.einsum("kac,kqc->aq", row_amps, fit_vectors, precision=highest)
            cycle_term = jnp.einsum("aq,jqb->jab", fitted, fit_vectors, precision=highest)
            ladder_term = jnp.zeros_like(row_amps)
            for factor_index in range(NL):
                factor = ladder_factors[factor_index]
                left_side = jnp.einsum("ac,jcd->jad", factor, row_amps, precision=highest)
                ladder_term = ladder_term + jnp.einsum("jad,bd->jab", left_side, factor, precision=highest)
            row_amps = (row_driver + cycle_term + ladder_term) / denominator
        return row_amps

    return lax.map(update_row, (amplitudes, driver, row_energy))
```

```python
import functools

import jax
import jax.numpy as jnp
from jax import lax
from jax.experimental import pallas as pl
from jax.experimental.pallas import tpu as pltpu
from jax.sharding import PartitionSpec as P

ITERS = 2
MESH = pl.DeviceIdType.MESH
F32 = jnp.float32
BF16 = jnp.bfloat16


def split(x):
    hi = x.astype(BF16)
    lo = (x - hi.astype(F32)).astype(BF16)
    return hi, lo


def mm(a, b):
    return lax.dot_general(a, b, (((1,), (0,)), ((), ())), preferred_element_type=F32)


def mm_t(a, b):
    return lax.dot_general(a, b, (((1,), (1,)), ((), ())), preferred_element_type=F32)


def left(hi, lo):
    return jnp.concatenate([hi, hi, lo], axis=1)


def kernel(
    sizes,
    amp_hbm, drv_hbm, fit_hbm, lad_hbm, row_e, occ_e, va_ref, vb_ref,
    out_hbm,
    gath, fh, fl, amp, acc, ah, al, lad, ch, cl, part, r1, r2, fit_sum, fth, ftl,
    s_in, s_out, s_ls, s_lr, s_zs, s_zr, s_ys, s_yr, s_n1, s_n2, s_n3,
):
    W, N, K, V, QB, NL, S = sizes
    Z = W // 2
    KS = K // S
    H = V // 2
    w = lax.axis_index("wide")
    n = lax.axis_index("narrow")
    z, y = w // 2, lax.rem(w, 2)
    core = lax.rem(n, 2)
    mate = n + 1 - 2 * core
    peers = N // 2 - 1

    own_fit = pltpu.make_async_copy(fit_hbm, gath.at[z, :, pl.ds(y * QB, QB), :], s_in.at[0])
    own_fit.start()
    rows = lad_hbm.shape[1]
    own_lad = pltpu.make_async_copy(lad_hbm, lad.at[:, pl.ds(w * rows, rows), :], s_in.at[1])
    own_lad.start()
    in_amp = pltpu.make_async_copy(amp_hbm.at[0], amp, s_in.at[2])
    in_amp.start()
    in_drv = [
        pltpu.make_async_copy(drv_hbm.at[0], acc.at[it], s_in.at[3 + it]) for it in range(ITERS)
    ]
    for cp in in_drv:
        cp.start()

    bar = pltpu.get_barrier_semaphore()
    for d in range(1, W):
        pl.semaphore_signal(bar, inc=1, device_id=(lax.rem(w + d, W), n), device_id_type=MESH)
    pl.semaphore_signal(bar, inc=1, device_id=(w, mate), device_id_type=MESH)
    for d in range(1, peers + 1):
        pl.semaphore_signal(bar, inc=1, device_id=(w, lax.rem(n + 2 * d, N)), device_id_type=MESH)
    pl.semaphore_wait(bar, W - 1 + 1 + peers)

    def place(zz, yy, r):
        return gath.at[zz, pl.ds(r * KS, KS), pl.ds(yy * QB, QB), :]

    def y_copy(zz, r):
        src = place(zz, y, r)
        return pltpu.make_async_remote_copy(
            src_ref=src, dst_ref=src, send_sem=s_ys.at[zz, r], recv_sem=s_yr.at[zz, r],
            device_id=(z * 2 + 1 - y, n), device_id_type=MESH)

    def y_recv(zz, r):
        dst = place(zz, 1 - y, r)
        return pltpu.make_async_remote_copy(
            src_ref=dst, dst_ref=dst, send_sem=s_ys.at[zz, r], recv_sem=s_yr.at[zz, r],
            device_id=(z * 2 + 1 - y, n), device_id_type=MESH)

    def z_copy(zz, r, up):
        last = r // S
        src = place(zz, y + last * (1 - 2 * y), r - last * S)
        to = z + 1 if up else z - 1
        return pltpu.make_async_remote_copy(
            src_ref=src, dst_ref=src, send_sem=s_zs.at[1 if up else 0, zz, r],
            recv_sem=s_zr.at[zz, r], device_id=(to * 2 + y, n), device_id_type=MESH)

    def lad_copy(d):
        src = lad.at[:, pl.ds(w * rows, rows), :]
        return pltpu.make_async_remote_copy(
            src_ref=src, dst_ref=src, send_sem=s_ls.at[d], recv_sem=s_lr.at[d],
            device_id=(lax.rem(w + d, W), n), device_id_type=MESH)

    def lad_recv(d):
        dst = lad.at[:, pl.ds(lax.rem(w + W - d, W) * rows, rows), :]
        return pltpu.make_async_remote_copy(
            src_ref=dst, dst_ref=dst, send_sem=s_ls.at[d], recv_sem=s_lr.at[d],
            device_id=(lax.rem(w + d, W), n), device_id_type=MESH)

    own_lad.wait()
    for d in range(1, W):
        lad_copy(d).start()
    own_fit.wait()

    def begin(r, carry):
        y_copy(z, r).start()

        @pl.when(z + 1 < Z)
        def _():
            z_copy(z, r, True).start()

        @pl.when(z > 0)
        def _():
            z_copy(z, r, False).start()
        return carry

    lax.fori_loop(0, S, begin, 0)

    in_amp.wait()

    def split_amp(k, carry):
        ah[k], al[k] = split(amp[k])
        return carry

    lax.fori_loop(0, K, split_amp, 0)

    y_recv(z, 0).wait_recv()

    @pl.when(z + 1 < Z)
    def _():
        z_copy(z, S, True).start()

    @pl.when(z > 0)
    def _():
        z_copy(z, S, False).start()

    for d in range(1, W):
        lad_recv(d).wait_recv()
    for p in range(NL):
        ch[p], cl[p] = split(lad[p])
    for cp in in_drv:
        cp.wait()

    def serve(s, r):
        def arrived(zz, up):
            z_copy(zz, r, up).wait_recv()

            @pl.when((z + 1 < Z) if up else (z > 0))
            def _():
                z_copy(zz, r, up).start()

            @pl.when((r >= 1) & (r < S))
            def _():
                y_copy(zz, r).start()

        @pl.when(z - 1 - s >= 0)
        def _():
            arrived(z - 1 - s, True)

        @pl.when(z + 1 + s < Z)
        def _():
            arrived(z + 1 + s, False)

    def ladder(it, k):
        th, tl = ah[k], al[k]
        right = jnp.concatenate([th, tl, th], axis=0)
        total = acc[it, k]
        for p in range(NL):
            xh, xl = split(mm(left(ch[p], cl[p]), right))
            total = total + mm_t(left(xh, xl), jnp.concatenate([ch[p], cl[p], ch[p]], axis=1))
        acc[it, k] = total

    def slot(m):
        low = jnp.minimum(z, Z - 1 - z)
        d_in = (m + 1) // 2
        sign_in = 1 if m % 2 == 0 else -1
        sign_out = jnp.where(z < Z - 1 - z, 1, -1)
        return jnp.where(m <= 2 * low, z + sign_in * d_in, z + sign_out * (m - low))

    def fitted_k(it, zz, k, first):
        if it == 0:
            bh, bl = split(gath[zz, k])
            fh[zz, k] = bh
            fl[zz, k] = bl
        else:
            bh, bl = fh[zz, k], fl[zz, k]
        got = mm_t(left(ah[k], al[k]), jnp.concatenate([bh, bl, bh], axis=1))
        part[it, zz] = jnp.where(first, got, part[it, zz] + got)

    def need(zz, r):
        @pl.when((r >= 1))
        def _():
            y_recv(zz, r).wait_recv()

    def fitted_piece(it, zz, r):
        if it == 0:
            need(zz, r)
        for q in range(KS):
            fitted_k(it, zz, r * KS + q, (r == 0) if q == 0 else False)

    mine = pl.ds(core * H, H)
    other = pl.ds((1 - core) * H, H)

    def n1(it, zz):
        return pltpu.make_async_remote_copy(
            src_ref=part.at[it, zz, other, :], dst_ref=r1.at[it, zz],
            send_sem=s_n1.at[0, it, zz], recv_sem=s_n1.at[1, it, zz],
            device_id=(w, mate), device_id_type=MESH)

    def n2(it, zz, d):
        return pltpu.make_async_remote_copy(
            src_ref=r2.at[it, zz, 0], dst_ref=r2.at[it, zz, d],
            send_sem=s_n2.at[0, it, zz, d - 1], recv_sem=s_n2.at[1, it, zz, d - 1],
            device_id=(w, lax.rem(n + 2 * d, N)), device_id_type=MESH)

    def n3(it, zz, half):
        ref = fit_sum.at[it, zz, half, :]
        return pltpu.make_async_remote_copy(
            src_ref=ref, dst_ref=ref,
            send_sem=s_n3.at[0, it, zz], recv_sem=s_n3.at[1, it, zz],
            device_id=(w, mate), device_id_type=MESH)

    def sum1(it, zz):
        n1(it, zz).wait_recv()
        r2[it, zz, 0] = part[it, zz, mine, :] + r1[it, zz]
        for d in range(1, peers + 1):
            n2(it, zz, d).start()

    def sum2(it, zz):
        total = r2[it, zz, 0]
        for d in range(1, peers + 1):
            n2(it, zz, d).wait_recv()
            total = total + r2[it, zz, d]
        fit_sum[it, zz, mine, :] = total
        n3(it, zz, mine).start()

    def sum3(it, zz):
        n3(it, zz, other).wait_recv()
        fth[zz], ftl[zz] = split(fit_sum[it, zz])

    def whole_slot(it, m):
        zz = slot(m)

        def body(r, carry):
            fitted_piece(it, zz, r)
            return carry

        lax.fori_loop(0, S, body, 0)
        n1(it, zz).start()

    pair = va_ref[...] + vb_ref[...]
    row = row_e[0]

    def finish(it, j, last):
        total = acc[it, j]
        for zz in range(Z):
            total = total + mm(
                left(fth[zz], ftl[zz]), jnp.concatenate([fh[zz, j], fl[zz, j], fh[zz, j]], axis=0))
        new = total / ((pair - row) - occ_e[j])
        if last:
            amp[j] = new
            pltpu.make_async_copy(amp.at[j], out_hbm.at[0, j], s_out.at[j]).start()
        else:
            ah[j], al[j] = split(new)

    for s in range(Z - 1):
        def tick(r, carry, s=s):
            serve(s, r)

            @pl.when(r < S)
            def _():
                if s == 0:
                    for q in range(KS):
                        ladder(0, r * KS + q)
                else:
                    fitted_piece(0, slot(s - 1), r)
            return carry

        lax.fori_loop(0, S + 1, tick, 0)
        if s > 0:
            n1(0, slot(s - 1)).start()
    for m in range(Z - 2, Z):
        whole_slot(0, m)

    for it in range(ITERS):
        if it > 0:
            for m in range(Z):
                whole_slot(it, m)
                if m > 0:
                    sum1(it, slot(m - 1))
                if m > 1:
                    sum2(it, slot(m - 2))
            sum1(it, slot(Z - 1))

            def lad_body(k, carry, it=it):
                ladder(it, k)
                return carry

            lax.fori_loop(0, K // 2, lad_body, 0)
            sum2(it, slot(Z - 2))
            sum2(it, slot(Z - 1))
            lax.fori_loop(K // 2, K, lad_body, 0)
            for m in range(Z):
                sum3(it, slot(m))
        else:
            for m in range(Z):
                sum1(it, slot(m))
            for m in range(Z):
                sum2(it, slot(m))
            for m in range(Z):
                sum3(it, slot(m))

        def fin_body(j, carry, it=it):
            finish(it, j, it == ITERS - 1)
            return carry

        lax.fori_loop(0, K, fin_body, 0)

    def out_body(j, carry):
        pltpu.make_async_copy(amp.at[j], out_hbm.at[0, j], s_out.at[j]).wait()
        return carry

    lax.fori_loop(0, K, out_body, 0)
    for d in range(1, W):
        lad_copy(d).wait_send()

    def end_y(r, carry):
        y_copy(z, r).wait_send()
        return carry

    lax.fori_loop(0, S, end_y, 0)

    def end_z(t, carry):
        zz, r = t // (S + 1), lax.rem(t, S + 1)

        @pl.when((zz <= z) & (z + 1 < Z))
        def _():
            z_copy(zz, r, True).wait_send()

        @pl.when((zz >= z) & (z > 0))
        def _():
            z_copy(zz, r, False).wait_send()

        @pl.when((zz != z) & (r >= 1) & (r < S))
        def _():
            y_copy(zz, r).wait_send()
        return carry

    lax.fori_loop(0, Z * (S + 1), end_z, 0)

    def end_n(zz, carry):
        for it in range(ITERS):
            n1(it, zz).wait_send()
            for d in range(1, peers + 1):
                n2(it, zz, d).wait_send()
            n3(it, zz, mine).wait_send()
        return carry

    lax.fori_loop(0, Z, end_n, 0)


def solution(mesh):
    W, N = mesh.shape["wide"], mesh.shape["narrow"]
    Z = W // 2

    def local(amplitudes, driver, fit, ladder, row_e, occ_e, virt):
        K, V = amplitudes.shape[1], amplitudes.shape[2]
        QB, NL = fit.shape[1], ladder.shape[0]
        S = max(K // 2, 1)
        QP = 2 * QB
        H = V // 2
        peers = N // 2 - 1
        any_ = pl.BlockSpec(memory_space=pl.ANY)
        smem = pl.BlockSpec(memory_space=pltpu.SMEM)
        vmem = pl.BlockSpec(memory_space=pltpu.VMEM)
        dma = pltpu.SemaphoreType.DMA
        return pl.pallas_call(
            functools.partial(kernel, (W, N, K, V, QB, NL, S)),
            out_shape=jax.ShapeDtypeStruct(amplitudes.shape, F32),
            in_specs=[any_, any_, any_, any_, smem, smem, vmem, vmem],
            out_specs=any_,
            scratch_shapes=[
                pltpu.VMEM((Z, K, QP, V), F32),
                pltpu.VMEM((Z, K, QP, V), BF16),
                pltpu.VMEM((Z, K, QP, V), BF16),
                pltpu.VMEM((K, V, V), F32),
                pltpu.VMEM((ITERS, K, V, V), F32),
                pltpu.VMEM((K, V, V), BF16),
                pltpu.VMEM((K, V, V), BF16),
                pltpu.VMEM((NL, V, V), F32),
                pltpu.VMEM((NL, V, V), BF16),
                pltpu.VMEM((NL, V, V), BF16),
                pltpu.VMEM((ITERS, Z, V, QP), F32),
                pltpu.VMEM((ITERS, Z, H, QP), F32),
                pltpu.VMEM((ITERS, Z, peers + 1, H, QP), F32),
                pltpu.VMEM((ITERS, Z, V, QP), F32),
                pltpu.VMEM((Z, V, QP), BF16),
                pltpu.VMEM((Z, V, QP), BF16),
                dma((3 + ITERS,)),
                dma((K,)),
                dma((W,)),
                dma((W,)),
                dma((2, Z, S + 1)),
                dma((Z, S + 1)),
                dma((Z, S)),
                dma((Z, S)),
                dma((2, ITERS, Z)),
                dma((2, ITERS, Z, peers)),
                dma((2, ITERS, Z)),
            ],
            compiler_params=pltpu.CompilerParams(
                collective_id=0, has_side_effects=True, vmem_limit_bytes=67043328),
        )(amplitudes, driver, fit, ladder, row_e, occ_e, virt[:, None], virt[None, :])

    placed = (
        P("wide", "narrow", None, None),
        P("wide", "narrow", None, None),
        P("narrow", "wide", None),
        P(None, "wide", None),
        P("wide"),
        P("narrow"),
        P(),
    )
    return jax.shard_map(
        local,
        mesh=mesh,
        in_specs=placed,
        out_specs=P("wide", "narrow", None, None),
        check_vma=False,
    )
```

```python
import functools

import jax
import jax.numpy as jnp
from jax import lax
from jax.experimental import pallas as pl
from jax.experimental.pallas import tpu as pltpu
from jax.sharding import PartitionSpec as P

ITERS = 2
MESH = pl.DeviceIdType.MESH
F32 = jnp.float32
BF16 = jnp.bfloat16


def split(x):
    hi = x.astype(BF16)
    lo = (x - hi.astype(F32)).astype(BF16)
    return hi, lo


def mm(a, b):
    return lax.dot_general(a, b, (((1,), (0,)), ((), ())), preferred_element_type=F32)


def mm_t(a, b):
    return lax.dot_general(a, b, (((1,), (1,)), ((), ())), preferred_element_type=F32)


def left(hi, lo):
    return jnp.concatenate([hi, hi, lo], axis=1)


def kernel(
    sizes,
    amp_hbm, drv_hbm, fit_hbm, lad_hbm, row_e, occ_e, va_ref, vb_ref,
    out_hbm,
    gath, fh, fl, amp, acc, ah, al, lad, ch, cl, part, r1, r2, fit_sum, fth, ftl,
    s_in, s_out, s_ls, s_lr, s_ns, s_nr, s_zs, s_zr, s_ys, s_yr, s_n1, s_n2, s_n3,
):
    W, N, K, V, QB, NL, S = sizes
    Z = W // 2
    KS = K // S
    H = V // 2
    w = lax.axis_index("wide")
    n = lax.axis_index("narrow")
    z, y = w // 2, lax.rem(w, 2)
    core = lax.rem(n, 2)
    mate = n + 1 - 2 * core
    peers = N // 2 - 1

    own_fit = pltpu.make_async_copy(fit_hbm, gath.at[z, :, pl.ds(y * QB, QB), :], s_in.at[0])
    own_fit.start()
    rows = lad_hbm.shape[1]
    D = lad.shape[2]
    share = lax.rem(n, D)
    rows_part = rows // D
    own_lad = pltpu.make_async_copy(
        lad_hbm.at[:, pl.ds(pl.multiple_of(share * rows_part, rows_part), rows_part), :],
        lad.at[:, w, share], s_in.at[1])
    own_lad.start()
    in_amp = pltpu.make_async_copy(amp_hbm.at[0], amp, s_in.at[2])
    in_drv = [
        pltpu.make_async_copy(drv_hbm.at[0], acc.at[it], s_in.at[3 + it]) for it in range(ITERS)
    ]

    bar = pltpu.get_barrier_semaphore()
    for d in range(1, W):
        pl.semaphore_signal(bar, inc=1, device_id=(lax.rem(w + d, W), n), device_id_type=MESH)
    for d in range(1, N):
        pl.semaphore_signal(bar, inc=1, device_id=(w, lax.rem(n + d, N)), device_id_type=MESH)
    pl.semaphore_wait(bar, W + N - 2)

    def place(zz, yy, r):
        return gath.at[zz, pl.ds(r * KS, KS), pl.ds(yy * QB, QB), :]

    def y_copy(zz, r):
        src = place(zz, y, r)
        return pltpu.make_async_remote_copy(
            src_ref=src, dst_ref=src, send_sem=s_ys.at[zz, r], recv_sem=s_yr.at[zz, r],
            device_id=(z * 2 + 1 - y, n), device_id_type=MESH)

    def y_recv(zz, r):
        dst = place(zz, 1 - y, r)
        return pltpu.make_async_remote_copy(
            src_ref=dst, dst_ref=dst, send_sem=s_ys.at[zz, r], recv_sem=s_yr.at[zz, r],
            device_id=(z * 2 + 1 - y, n), device_id_type=MESH)

    def z_copy(zz, r, up):
        last = r // S
        src = place(zz, y + last * (1 - 2 * y), r - last * S)
        to = z + 1 if up else z - 1
        return pltpu.make_async_remote_copy(
            src_ref=src, dst_ref=src, send_sem=s_zs.at[1 if up else 0, zz, r],
            recv_sem=s_zr.at[zz, r], device_id=(to * 2 + y, n), device_id_type=MESH)

    def lad_copy(d):
        src = lad.at[:, w, share]
        return pltpu.make_async_remote_copy(
            src_ref=src, dst_ref=src, send_sem=s_ls.at[d], recv_sem=s_lr.at[d],
            device_id=(lax.rem(w + d, W), n), device_id_type=MESH)

    def lad_recv(d):
        dst = lad.at[:, lax.rem(w + W - d, W), share]
        return pltpu.make_async_remote_copy(
            src_ref=dst, dst_ref=dst, send_sem=s_ls.at[d], recv_sem=s_lr.at[d],
            device_id=(lax.rem(w + d, W), n), device_id_type=MESH)

    own_fit.wait()
    own_lad.wait()

    def lad_spread(d, mine):
        part_of = share if mine else lax.rem(share + D - d, D)
        ref = lad.at[:, :, part_of]
        return pltpu.make_async_remote_copy(
            src_ref=ref, dst_ref=ref, send_sem=s_ns.at[d], recv_sem=s_nr.at[d],
            device_id=(w, n - share + lax.rem(share + d, D)), device_id_type=MESH)


    def begin(r, carry):
        y_copy(z, r).start()

        @pl.when(z + 1 < Z)
        def _():
            z_copy(z, r, True).start()

        @pl.when(z > 0)
        def _():
            z_copy(z, r, False).start()
        return carry

    begin(0, 0)
    for d in range(1, W):
        lad_copy(d).start()
    lax.fori_loop(1, S, begin, 0)
    in_amp.start()
    for cp in in_drv:
        cp.start()

    in_amp.wait()

    def split_amp(k, carry):
        ah[k], al[k] = split(amp[k])
        return carry

    lax.fori_loop(0, K, split_amp, 0)

    y_recv(z, 0).wait_recv()

    @pl.when(z + 1 < Z)
    def _():
        z_copy(z, S, True).start()

    @pl.when(z > 0)
    def _():
        z_copy(z, S, False).start()

    for d in range(1, W):
        lad_recv(d).wait_recv()
    for d in range(1, D):
        lad_spread(d, True).start()
    for d in range(1, D):
        lad_spread(d, False).wait_recv()
    for p in range(NL):
        ch[p], cl[p] = split(lad[p].reshape(V, V))
    for cp in in_drv:
        cp.wait()

    def serve(s, r):
        def arrived(zz, up):
            z_copy(zz, r, up).wait_recv()

            @pl.when((z + 1 < Z) if up else (z > 0))
            def _():
                z_copy(zz, r, up).start()

            @pl.when((r >= 1) & (r < S))
            def _():
                y_copy(zz, r).start()

        @pl.when(z - 1 - s >= 0)
        def _():
            arrived(z - 1 - s, True)

        @pl.when(z + 1 + s < Z)
        def _():
            arrived(z + 1 + s, False)

    def ladder(it, k):
        th, tl = ah[k], al[k]
        right = jnp.concatenate([th, tl, th], axis=0)
        total = acc[it, k]
        for p in range(NL):
            xh, xl = split(mm(left(ch[p], cl[p]), right))
            total = total + mm_t(left(xh, xl), jnp.concatenate([ch[p], cl[p], ch[p]], axis=1))
        acc[it, k] = total

    def slot(m):
        low = jnp.minimum(z, Z - 1 - z)
        d_in = (m + 1) // 2
        sign_in = 1 if m % 2 == 0 else -1
        sign_out = jnp.where(z < Z - 1 - z, 1, -1)
        return jnp.where(m <= 2 * low, z + sign_in * d_in, z + sign_out * (m - low))

    def fitted_k(it, zz, k, first):
        if it == 0:
            bh, bl = split(gath[zz, k])
            fh[zz, k] = bh
            fl[zz, k] = bl
        else:
            bh, bl = fh[zz, k], fl[zz, k]
        got = mm_t(left(ah[k], al[k]), jnp.concatenate([bh, bl, bh], axis=1))
        part[it, zz] = jnp.where(first, got, part[it, zz] + got)

    def need(zz, r):
        @pl.when((r >= 1))
        def _():
            y_recv(zz, r).wait_recv()

    def fitted_piece(it, zz, r):
        if it == 0:
            need(zz, r)
        for q in range(KS):
            fitted_k(it, zz, r * KS + q, (r == 0) if q == 0 else False)

    mine = pl.ds(core * H, H)
    other = pl.ds((1 - core) * H, H)

    def n1(it, zz):
        return pltpu.make_async_remote_copy(
            src_ref=part.at[it, zz, other, :], dst_ref=r1.at[it, zz],
            send_sem=s_n1.at[0, it, zz], recv_sem=s_n1.at[1, it, zz],
            device_id=(w, mate), device_id_type=MESH)

    def n2(it, zz, d):
        return pltpu.make_async_remote_copy(
            src_ref=r2.at[it, zz, 0], dst_ref=r2.at[it, zz, d],
            send_sem=s_n2.at[0, it, zz, d - 1], recv_sem=s_n2.at[1, it, zz, d - 1],
            device_id=(w, lax.rem(n + 2 * d, N)), device_id_type=MESH)

    def n3(it, zz, half):
        ref = fit_sum.at[it, zz, half, :]
        return pltpu.make_async_remote_copy(
            src_ref=ref, dst_ref=ref,
            send_sem=s_n3.at[0, it, zz], recv_sem=s_n3.at[1, it, zz],
            device_id=(w, mate), device_id_type=MESH)

    def sum1(it, zz):
        n1(it, zz).wait_recv()
        r2[it, zz, 0] = part[it, zz, mine, :] + r1[it, zz]
        for d in range(1, peers + 1):
            n2(it, zz, d).start()

    def sum2(it, zz):
        total = r2[it, zz, 0]
        for d in range(1, peers + 1):
            n2(it, zz, d).wait_recv()
            total = total + r2[it, zz, d]
        fit_sum[it, zz, mine, :] = total
        n3(it, zz, mine).start()

    def sum3(it, zz):
        n3(it, zz, other).wait_recv()
        fth[zz], ftl[zz] = split(fit_sum[it, zz])

    def whole_slot(it, m):
        zz = slot(m)

        def body(r, carry):
            fitted_piece(it, zz, r)
            return carry

        lax.fori_loop(0, S, body, 0)
        n1(it, zz).start()

    pair = va_ref[...] + vb_ref[...]
    row = row_e[0]

    def cycle(zz, j):
        return mm(
            left(fth[zz], ftl[zz]), jnp.concatenate([fh[zz, j], fl[zz, j], fh[zz, j]], axis=0))

    def cycles(it, slots):
        def body(j, carry):
            total = acc[it, j]
            for m in slots:
                total = total + cycle(slot(m), j)
            acc[it, j] = total
            return carry

        lax.fori_loop(0, K, body, 0)

    def finish(it, j, slots, last):
        total = acc[it, j]
        for m in slots:
            total = total + cycle(slot(m), j)
        new = total / ((pair - row) - occ_e[j])
        if last:
            amp[j] = new
            pltpu.make_async_copy(amp.at[j], out_hbm.at[0, j], s_out.at[j]).start()
        else:
            ah[j], al[j] = split(new)

    def finish_all(it, slots):
        def body(j, carry):
            finish(it, j, slots, it == ITERS - 1)
            return carry

        lax.fori_loop(0, K, body, 0)

    def sums(it, slots):
        for m in slots:
            sum1(it, slot(m))
        for m in slots:
            sum2(it, slot(m))
        for m in slots:
            sum3(it, slot(m))

    for s in range(Z - 1):
        def tick(r, carry, s=s):
            serve(s, r)

            @pl.when(r < S)
            def _():
                if s == 0:
                    for q in range(KS):
                        ladder(0, r * KS + q)
                else:
                    fitted_piece(0, slot(s - 1), r)
            if s > 1:
                zz = slot(s - 2)
                for at, stage in ((0, sum1), (S // 2, sum2), (S, sum3)):
                    @pl.when(r == at)
                    def _(stage=stage, zz=zz):
                        stage(0, zz)
            return carry

        lax.fori_loop(0, S + 1, tick, 0)
        if s > 0:
            n1(0, slot(s - 1)).start()
    summed = max(Z - 3, 0)
    if Z > 1:
        whole_slot(0, Z - 2)
    if summed > 0:
        cycles(0, range(summed))
    sums(0, range(summed, Z - 1))
    if Z > 1:
        cycles(0, range(summed, Z - 1))
    whole_slot(0, Z - 1)
    sums(0, [Z - 1])
    finish_all(0, [Z - 1])

    for it in range(1, ITERS):
        for m in range(Z):
            whole_slot(it, m)
            if m > 0:
                sum1(it, slot(m - 1))

        def lad_body(k, carry, it=it):
            ladder(it, k)
            return carry

        half = Z // 2
        lax.fori_loop(0, K // 4, lad_body, 0)
        sum1(it, slot(Z - 1))
        lax.fori_loop(K // 4, K - K // 4, lad_body, 0)
        for m in range(half):
            sum2(it, slot(m))
        lax.fori_loop(K - K // 4, K, lad_body, 0)
        for m in range(half):
            sum3(it, slot(m))
        if half > 0:
            cycles(it, range(half))
        for m in range(half, Z - 1):
            sum2(it, slot(m))
        for m in range(half, Z - 1):
            sum3(it, slot(m))
        if half < Z - 1:
            cycles(it, range(half, Z - 1))
        sum2(it, slot(Z - 1))
        sum3(it, slot(Z - 1))
        finish_all(it, [Z - 1])

    def out_body(j, carry):
        pltpu.make_async_copy(amp.at[j], out_hbm.at[0, j], s_out.at[j]).wait()
        return carry

    lax.fori_loop(0, K, out_body, 0)
    for d in range(1, W):
        lad_copy(d).wait_send()
    for d in range(1, D):
        lad_spread(d, True).wait_send()

    def end_y(r, carry):
        y_copy(z, r).wait_send()
        return carry

    lax.fori_loop(0, S, end_y, 0)

    def end_z(t, carry):
        zz, r = t // (S + 1), lax.rem(t, S + 1)

        @pl.when((zz <= z) & (z + 1 < Z))
        def _():
            z_copy(zz, r, True).wait_send()

        @pl.when((zz >= z) & (z > 0))
        def _():
            z_copy(zz, r, False).wait_send()

        @pl.when((zz != z) & (r >= 1) & (r < S))
        def _():
            y_copy(zz, r).wait_send()
        return carry

    lax.fori_loop(0, Z * (S + 1), end_z, 0)

    def end_n(zz, carry):
        for it in range(ITERS):
            n1(it, zz).wait_send()
            for d in range(1, peers + 1):
                n2(it, zz, d).wait_send()
            n3(it, zz, mine).wait_send()
        return carry

    lax.fori_loop(0, Z, end_n, 0)


def solution(mesh):
    W, N = mesh.shape["wide"], mesh.shape["narrow"]
    Z = W // 2

    def local(amplitudes, driver, fit, ladder, row_e, occ_e, virt):
        K, V = amplitudes.shape[1], amplitudes.shape[2]
        QB, NL = fit.shape[1], ladder.shape[0]
        S = max(K // 2, 1)
        QP = 2 * QB
        rows = ladder.shape[1]
        D = 1
        while N % (2 * D) == 0 and rows % (16 * D) == 0:
            D *= 2
        H = V // 2
        peers = N // 2 - 1
        any_ = pl.BlockSpec(memory_space=pl.ANY)
        smem = pl.BlockSpec(memory_space=pltpu.SMEM)
        vmem = pl.BlockSpec(memory_space=pltpu.VMEM)
        dma = pltpu.SemaphoreType.DMA
        return pl.pallas_call(
            functools.partial(kernel, (W, N, K, V, QB, NL, S)),
            out_shape=jax.ShapeDtypeStruct(amplitudes.shape, F32),
            in_specs=[any_, any_, any_, any_, smem, smem, vmem, vmem],
            out_specs=any_,
            scratch_shapes=[
                pltpu.VMEM((Z, K, QP, V), F32),
                pltpu.VMEM((Z, K, QP, V), BF16),
                pltpu.VMEM((Z, K, QP, V), BF16),
                pltpu.VMEM((K, V, V), F32),
                pltpu.VMEM((ITERS, K, V, V), F32),
                pltpu.VMEM((K, V, V), BF16),
                pltpu.VMEM((K, V, V), BF16),
                pltpu.VMEM((NL, W, D, rows // D, V), F32),
                pltpu.VMEM((NL, V, V), BF16),
                pltpu.VMEM((NL, V, V), BF16),
                pltpu.VMEM((ITERS, Z, V, QP), F32),
                pltpu.VMEM((ITERS, Z, H, QP), F32),
                pltpu.VMEM((ITERS, Z, peers + 1, H, QP), F32),
                pltpu.VMEM((ITERS, Z, V, QP), F32),
                pltpu.VMEM((Z, V, QP), BF16),
                pltpu.VMEM((Z, V, QP), BF16),
                dma((3 + ITERS,)),
                dma((K,)),
                dma((W,)),
                dma((W,)),
                dma((D,)),
                dma((D,)),
                dma((2, Z, S + 1)),
                dma((Z, S + 1)),
                dma((Z, S)),
                dma((Z, S)),
                dma((2, ITERS, Z)),
                dma((2, ITERS, Z, peers)),
                dma((2, ITERS, Z)),
            ],
            compiler_params=pltpu.CompilerParams(
                collective_id=0, has_side_effects=True, vmem_limit_bytes=67043328),
        )(amplitudes, driver, fit, ladder, row_e, occ_e, virt[:, None], virt[None, :])

    placed = (
        P("wide", "narrow", None, None),
        P("wide", "narrow", None, None),
        P("narrow", "wide", None),
        P(None, "wide", None),
        P("wide"),
        P("narrow"),
        P(),
    )
    return jax.shard_map(
        local,
        mesh=mesh,
        in_specs=placed,
        out_specs=P("wide", "narrow", None, None),
        check_vma=False,
    )
```

```python
import functools

import jax
import jax.numpy as jnp
from jax import lax
from jax.experimental import pallas as pl
from jax.experimental.pallas import tpu as pltpu
from jax.sharding import PartitionSpec as P

ITERS = 2
MESH = pl.DeviceIdType.MESH
F32 = jnp.float32
BF16 = jnp.bfloat16


def split(x):
    hi = x.astype(BF16)
    lo = (x - hi.astype(F32)).astype(BF16)
    return hi, lo


def mm(a, b):
    return lax.dot_general(a, b, (((1,), (0,)), ((), ())), preferred_element_type=F32)


def mm_t(a, b):
    return lax.dot_general(a, b, (((1,), (1,)), ((), ())), preferred_element_type=F32)


def left(hi, lo):
    return jnp.concatenate([hi, hi, lo], axis=1)


def kernel(
    sizes,
    amp_hbm, drv_hbm, fit_hbm, lad_hbm, row_e, occ_e, va_ref, vb_ref,
    out_hbm,
    gath, fh, fl, amp, acc, ah, al, lad, ch, cl, part, r1, r2, fit_sum, fth, ftl,
    s_in, s_out, s_ls, s_lr, s_ns, s_nr, s_zs, s_zr, s_ys, s_yr, s_n1, s_n2, s_n3,
):
    W, N, K, V, QB, NL, S = sizes
    Z = W // 2
    KS = K // S
    H = V // 2
    w = lax.axis_index("wide")
    n = lax.axis_index("narrow")
    z, y = w // 2, lax.rem(w, 2)
    core = lax.rem(n, 2)
    mate = n + 1 - 2 * core
    peers = N // 2 - 1

    own_fit = pltpu.make_async_copy(fit_hbm, gath.at[z, :, pl.ds(y * QB, QB), :], s_in.at[0])
    own_fit.start()
    rows = lad_hbm.shape[1]
    D = lad.shape[2]
    share = lax.rem(n, D)
    rows_part = rows // D
    own_lad = pltpu.make_async_copy(
        lad_hbm.at[:, pl.ds(pl.multiple_of(share * rows_part, rows_part), rows_part), :],
        lad.at[:, w, share], s_in.at[1])
    own_lad.start()
    in_amp = pltpu.make_async_copy(amp_hbm.at[0], amp, s_in.at[2])
    in_drv = [
        pltpu.make_async_copy(drv_hbm.at[0], acc.at[it], s_in.at[3 + it]) for it in range(ITERS)
    ]

    bar = pltpu.get_barrier_semaphore()
    for d in range(1, W):
        pl.semaphore_signal(bar, inc=1, device_id=(lax.rem(w + d, W), n), device_id_type=MESH)
    for d in range(1, N):
        pl.semaphore_signal(bar, inc=1, device_id=(w, lax.rem(n + d, N)), device_id_type=MESH)
    pl.semaphore_wait(bar, W + N - 2)

    def place(zz, yy, r):
        return gath.at[zz, pl.ds(r * KS, KS), pl.ds(yy * QB, QB), :]

    def y_copy(zz, r):
        src = place(zz, y, r)
        return pltpu.make_async_remote_copy(
            src_ref=src, dst_ref=src, send_sem=s_ys.at[zz, r], recv_sem=s_yr.at[zz, r],
            device_id=(z * 2 + 1 - y, n), device_id_type=MESH)

    def y_recv(zz, r):
        dst = place(zz, 1 - y, r)
        return pltpu.make_async_remote_copy(
            src_ref=dst, dst_ref=dst, send_sem=s_ys.at[zz, r], recv_sem=s_yr.at[zz, r],
            device_id=(z * 2 + 1 - y, n), device_id_type=MESH)

    def z_copy(zz, r, up):
        last = r // S
        src = place(zz, y + last * (1 - 2 * y), r - last * S)
        to = z + 1 if up else z - 1
        return pltpu.make_async_remote_copy(
            src_ref=src, dst_ref=src, send_sem=s_zs.at[1 if up else 0, zz, r],
            recv_sem=s_zr.at[zz, r], device_id=(to * 2 + y, n), device_id_type=MESH)

    def lad_copy(d):
        src = lad.at[:, w, share]
        return pltpu.make_async_remote_copy(
            src_ref=src, dst_ref=src, send_sem=s_ls.at[d], recv_sem=s_lr.at[d],
            device_id=(lax.rem(w + d, W), n), device_id_type=MESH)

    def lad_recv(d):
        dst = lad.at[:, lax.rem(w + W - d, W), share]
        return pltpu.make_async_remote_copy(
            src_ref=dst, dst_ref=dst, send_sem=s_ls.at[d], recv_sem=s_lr.at[d],
            device_id=(lax.rem(w + d, W), n), device_id_type=MESH)

    own_fit.wait()
    own_lad.wait()

    def lad_spread(d, mine):
        part_of = share if mine else lax.rem(share + D - d, D)
        ref = lad.at[:, :, part_of]
        return pltpu.make_async_remote_copy(
            src_ref=ref, dst_ref=ref, send_sem=s_ns.at[d], recv_sem=s_nr.at[d],
            device_id=(w, n - share + lax.rem(share + d, D)), device_id_type=MESH)


    def begin(r, carry):
        y_copy(z, r).start()

        @pl.when(z + 1 < Z)
        def _():
            z_copy(z, r, True).start()

        @pl.when(z > 0)
        def _():
            z_copy(z, r, False).start()
        return carry

    begin(0, 0)
    for d in range(1, W):
        lad_copy(d).start()
    lax.fori_loop(1, S, begin, 0)
    in_amp.start()
    for cp in in_drv:
        cp.start()

    in_amp.wait()

    def split_amp(k, carry):
        ah[k], al[k] = split(amp[k])
        return carry

    lax.fori_loop(0, K, split_amp, 0)

    y_recv(z, 0).wait_recv()

    @pl.when(z + 1 < Z)
    def _():
        z_copy(z, S, True).start()

    @pl.when(z > 0)
    def _():
        z_copy(z, S, False).start()

    for d in range(1, W):
        lad_recv(d).wait_recv()
    for d in range(1, D):
        lad_spread(d, True).start()
    for d in range(1, D):
        lad_spread(d, False).wait_recv()
    for p in range(NL):
        ch[p], cl[p] = split(lad[p].reshape(V, V))
    for cp in in_drv:
        cp.wait()

    def serve(s, r):
        def arrived(zz, up):
            z_copy(zz, r, up).wait_recv()

            @pl.when((z + 1 < Z) if up else (z > 0))
            def _():
                z_copy(zz, r, up).start()

            @pl.when((r >= 1) & (r < S))
            def _():
                y_copy(zz, r).start()

        @pl.when(z - 1 - s >= 0)
        def _():
            arrived(z - 1 - s, True)

        @pl.when(z + 1 + s < Z)
        def _():
            arrived(z + 1 + s, False)

    def ladder(it, k):
        th, tl = ah[k], al[k]
        right = jnp.concatenate([th, tl, th], axis=0)
        total = acc[it, k]
        for p in range(NL):
            xh, xl = split(mm(left(ch[p], cl[p]), right))
            total = total + mm_t(left(xh, xl), jnp.concatenate([ch[p], cl[p], ch[p]], axis=1))
        acc[it, k] = total

    def slot(m):
        low = jnp.minimum(z, Z - 1 - z)
        d_in = (m + 1) // 2
        sign_in = 1 if m % 2 == 0 else -1
        sign_out = jnp.where(z < Z - 1 - z, 1, -1)
        return jnp.where(m <= 2 * low, z + sign_in * d_in, z + sign_out * (m - low))

    def fitted_k(it, zz, k, first):
        if it == 0:
            bh, bl = split(gath[zz, k])
            fh[zz, k] = bh
            fl[zz, k] = bl
        else:
            bh, bl = fh[zz, k], fl[zz, k]
        got = mm_t(left(ah[k], al[k]), jnp.concatenate([bh, bl, bh], axis=1))
        part[it, zz] = jnp.where(first, got, part[it, zz] + got)

    def need(zz, r):
        @pl.when((r >= 1))
        def _():
            y_recv(zz, r).wait_recv()

    def fitted_piece(it, zz, r):
        if it == 0:
            need(zz, r)
        for q in range(KS):
            fitted_k(it, zz, r * KS + q, (r == 0) if q == 0 else False)

    mine = pl.ds(core * H, H)
    other = pl.ds((1 - core) * H, H)

    def n1(it, zz):
        return pltpu.make_async_remote_copy(
            src_ref=part.at[it, zz, other, :], dst_ref=r1.at[it, zz],
            send_sem=s_n1.at[0, it, zz], recv_sem=s_n1.at[1, it, zz],
            device_id=(w, mate), device_id_type=MESH)

    def n2(it, zz, d):
        return pltpu.make_async_remote_copy(
            src_ref=r2.at[it, zz, 0], dst_ref=r2.at[it, zz, d],
            send_sem=s_n2.at[0, it, zz, d - 1], recv_sem=s_n2.at[1, it, zz, d - 1],
            device_id=(w, lax.rem(n + 2 * d, N)), device_id_type=MESH)

    def n3(it, zz, half):
        ref = fit_sum.at[it, zz, half, :]
        return pltpu.make_async_remote_copy(
            src_ref=ref, dst_ref=ref,
            send_sem=s_n3.at[0, it, zz], recv_sem=s_n3.at[1, it, zz],
            device_id=(w, mate), device_id_type=MESH)

    def sum1(it, zz):
        n1(it, zz).wait_recv()
        r2[it, zz, 0] = part[it, zz, mine, :] + r1[it, zz]
        for d in range(1, peers + 1):
            n2(it, zz, d).start()

    def sum2(it, zz):
        total = r2[it, zz, 0]
        for d in range(1, peers + 1):
            n2(it, zz, d).wait_recv()
            total = total + r2[it, zz, d]
        fit_sum[it, zz, mine, :] = total
        n3(it, zz, mine).start()

    def sum3(it, zz):
        n3(it, zz, other).wait_recv()
        fth[zz], ftl[zz] = split(fit_sum[it, zz])

    def whole_slot(it, m):
        zz = slot(m)

        def body(r, carry):
            fitted_piece(it, zz, r)
            return carry

        lax.fori_loop(0, S, body, 0)
        n1(it, zz).start()

    pair = va_ref[...] + vb_ref[...]
    row = row_e[0]

    def finish(it, j, last):
        total = acc[it, j]
        for zz in range(Z):
            total = total + mm(
                left(fth[zz], ftl[zz]), jnp.concatenate([fh[zz, j], fl[zz, j], fh[zz, j]], axis=0))
        new = total / ((pair - row) - occ_e[j])
        if last:
            amp[j] = new
            pltpu.make_async_copy(amp.at[j], out_hbm.at[0, j], s_out.at[j]).start()
        else:
            ah[j], al[j] = split(new)

    for s in range(Z - 1):
        def tick(r, carry, s=s):
            serve(s, r)

            @pl.when(r < S)
            def _():
                if s == 0:
                    for q in range(KS):
                        ladder(0, r * KS + q)
                else:
                    fitted_piece(0, slot(s - 1), r)
            return carry

        lax.fori_loop(0, S + 1, tick, 0)
        if s > 0:
            n1(0, slot(s - 1)).start()
    for m in range(Z - 2, Z):
        whole_slot(0, m)

    for it in range(ITERS):
        if it > 0:
            for m in range(Z):
                whole_slot(it, m)
                if m > 0:
                    sum1(it, slot(m - 1))
                if m > 1:
                    sum2(it, slot(m - 2))
            sum1(it, slot(Z - 1))

            def lad_body(k, carry, it=it):
                ladder(it, k)
                return carry

            lax.fori_loop(0, K // 2, lad_body, 0)
            sum2(it, slot(Z - 2))
            sum2(it, slot(Z - 1))
            lax.fori_loop(K // 2, K, lad_body, 0)
            for m in range(Z):
                sum3(it, slot(m))
        else:
            for m in range(Z):
                sum1(it, slot(m))
            for m in range(Z):
                sum2(it, slot(m))
            for m in range(Z):
                sum3(it, slot(m))

        def fin_body(j, carry, it=it):
            finish(it, j, it == ITERS - 1)
            return carry

        lax.fori_loop(0, K, fin_body, 0)

    def out_body(j, carry):
        pltpu.make_async_copy(amp.at[j], out_hbm.at[0, j], s_out.at[j]).wait()
        return carry

    lax.fori_loop(0, K, out_body, 0)
    for d in range(1, W):
        lad_copy(d).wait_send()
    for d in range(1, D):
        lad_spread(d, True).wait_send()

    def end_y(r, carry):
        y_copy(z, r).wait_send()
        return carry

    lax.fori_loop(0, S, end_y, 0)

    def end_z(t, carry):
        zz, r = t // (S + 1), lax.rem(t, S + 1)

        @pl.when((zz <= z) & (z + 1 < Z))
        def _():
            z_copy(zz, r, True).wait_send()

        @pl.when((zz >= z) & (z > 0))
        def _():
            z_copy(zz, r, False).wait_send()

        @pl.when((zz != z) & (r >= 1) & (r < S))
        def _():
            y_copy(zz, r).wait_send()
        return carry

    lax.fori_loop(0, Z * (S + 1), end_z, 0)

    def end_n(zz, carry):
        for it in range(ITERS):
            n1(it, zz).wait_send()
            for d in range(1, peers + 1):
                n2(it, zz, d).wait_send()
            n3(it, zz, mine).wait_send()
        return carry

    lax.fori_loop(0, Z, end_n, 0)


def solution(mesh):
    W, N = mesh.shape["wide"], mesh.shape["narrow"]
    Z = W // 2

    def local(amplitudes, driver, fit, ladder, row_e, occ_e, virt):
        K, V = amplitudes.shape[1], amplitudes.shape[2]
        QB, NL = fit.shape[1], ladder.shape[0]
        S = max(K // 2, 1)
        QP = 2 * QB
        rows = ladder.shape[1]
        D = 1
        while N % (2 * D) == 0 and rows % (16 * D) == 0:
            D *= 2
        H = V // 2
        peers = N // 2 - 1
        any_ = pl.BlockSpec(memory_space=pl.ANY)
        smem = pl.BlockSpec(memory_space=pltpu.SMEM)
        vmem = pl.BlockSpec(memory_space=pltpu.VMEM)
        dma = pltpu.SemaphoreType.DMA
        return pl.pallas_call(
            functools.partial(kernel, (W, N, K, V, QB, NL, S)),
            out_shape=jax.ShapeDtypeStruct(amplitudes.shape, F32),
            in_specs=[any_, any_, any_, any_, smem, smem, vmem, vmem],
            out_specs=any_,
            scratch_shapes=[
                pltpu.VMEM((Z, K, QP, V), F32),
                pltpu.VMEM((Z, K, QP, V), BF16),
                pltpu.VMEM((Z, K, QP, V), BF16),
                pltpu.VMEM((K, V, V), F32),
                pltpu.VMEM((ITERS, K, V, V), F32),
                pltpu.VMEM((K, V, V), BF16),
                pltpu.VMEM((K, V, V), BF16),
                pltpu.VMEM((NL, W, D, rows // D, V), F32),
                pltpu.VMEM((NL, V, V), BF16),
                pltpu.VMEM((NL, V, V), BF16),
                pltpu.VMEM((ITERS, Z, V, QP), F32),
                pltpu.VMEM((ITERS, Z, H, QP), F32),
                pltpu.VMEM((ITERS, Z, peers + 1, H, QP), F32),
                pltpu.VMEM((ITERS, Z, V, QP), F32),
                pltpu.VMEM((Z, V, QP), BF16),
                pltpu.VMEM((Z, V, QP), BF16),
                dma((3 + ITERS,)),
                dma((K,)),
                dma((W,)),
                dma((W,)),
                dma((D,)),
                dma((D,)),
                dma((2, Z, S + 1)),
                dma((Z, S + 1)),
                dma((Z, S)),
                dma((Z, S)),
                dma((2, ITERS, Z)),
                dma((2, ITERS, Z, peers)),
                dma((2, ITERS, Z)),
            ],
            compiler_params=pltpu.CompilerParams(
                collective_id=0, has_side_effects=True, vmem_limit_bytes=67043328),
        )(amplitudes, driver, fit, ladder, row_e, occ_e, virt[:, None], virt[None, :])

    placed = (
        P("wide", "narrow", None, None),
        P("wide", "narrow", None, None),
        P("narrow", "wide", None),
        P(None, "wide", None),
        P("wide"),
        P("narrow"),
        P(),
    )
    return jax.shard_map(
        local,
        mesh=mesh,
        in_specs=placed,
        out_specs=P("wide", "narrow", None, None),
        check_vma=False,
    )
```
